32 devices in a mesh: dom: 16 (over z, y, x), sub: 2 (over core).
Axes of the slice: x: 2, y: 2, z: 4, core: 2. Of those that a mesh axis runs over, the one named last changes fastest.
Arguments:
- positions: float32 [3, 262144], P(None, ('dom', 'sub')), may hold values from -6 to 6
- masses: float32 [262144], P(('dom', 'sub')), may hold values from 0.0005 to 0.005
- old_accel: float32 [3, 262144], P(None, ('dom', 'sub')), may hold values from -6 to 6
- active: int32 [1024], P('dom'), may hold values from 0 to 1, as said below
- parent_of: int32 [1024], P(('dom', 'sub')), may hold values from 0 to 255
- parent_centers: float32 [3, 256], replicated, may hold values from -4 to 4
- local_list: int32 [1024, 8], P('dom'), may hold values from 0 to 63
- near_list: int32 [1024, 8], P('dom'), may hold values from 0 to 127, as said below
- far_list: int32 [1024, 16], P('dom'), may hold values from 0 to 255, as said below
- send_ids: int32 [32, 16, 4], P(('dom', 'sub')), may hold values from -1 to 31, as said below
- cell_send_ids: int32 [32, 16, 8], P(('dom', 'sub')), may hold values from -1 to 31, as said below
Outputs:
- accel: float32 [3, 262144], P(None, ('dom', 'sub'))
- parent_moments: float32 [35, 256], P(None, 'dom')
The draws below stay inside these ranges and needn't reach their ends.
Inputs may be any that keep to these rules, and one draw needn't show every extreme that they name: On each device between 1 and 16 of its 32 groups are active, and on some device exactly 16. For device g and chip c, slots 0 to n - 1 of send_ids[g, c] name groups of device g and the others hold -1, with 1 <= n <= 4; n = 4 and n = 1 occur in every draw. For device g and chip c, slots 0 to n - 1 of cell_send_ids[g, c] name groups of device g and the others hold -1, with 1 <= n <= 8; n = 8 and n = 1 occur in every draw. `near_list`: an entry g * 4 + k names slot k of send_ids[g, c], c the chip of the row's group; that slot is never -1. `far_list`: an entry g * 8 + k names slot k of cell_send_ids[g, c], c the chip of the row's group; that slot is never -1.
All inputs are finite; a program needn't handle non-finite values.
Results may differ from the reference program's by a relative error of at most 0.0003.
Values sent between devices are 32-bit elements; how exact they have to be, the bound alone decides.
A program may use at most 64 MiB of HBM per device.

```python
import math
import jax
import jax.numpy as jnp
import numpy as np
from jax import lax

BUCKET = 256
NB = 32
LOCAL_N = 8
NEAR = 8
FAR = 16
RQ = 4
RQC = 8
ACT_MAX = 16
CHIPS = 16
CORES = 32
BUCKETS = 1024
PARTICLES = 262144
NPAR = 256


def slot_counts(key, capacity, salt):
    count_key, spot_key = jax.random.split(jax.random.fold_in(key, salt))
    counts = jax.random.randint(count_key, (CORES, CHIPS), 1, capacity + 1)
    places = jnp.arange(CORES * CHIPS, dtype=jnp.int32).reshape(CORES, CHIPS)
    full_spot = jax.random.randint(spot_key, (), 0, CORES * CHIPS)
    thin_spot = (full_spot + CHIPS) % (CORES * CHIPS)
    counts = jnp.where(places == thin_spot, 1, counts)
    return jnp.where(places == full_spot, capacity, counts)


def send_table(key, capacity, count_salt, pick_salt):
    counts = slot_counts(key, capacity, count_salt)
    chosen = jax.random.randint(jax.random.fold_in(key, pick_salt), (CORES, CHIPS, capacity), 0, NB)
    slot_places = jnp.arange(capacity, dtype=jnp.int32)
    return jnp.where(slot_places[None, None, :] < counts[:, :, None], chosen, -1).astype(jnp.int32)


def list_table(key, capacity, count_salt, list_salt, width):
    counts = slot_counts(key, capacity, count_salt)
    source_key, slot_key = jax.random.split(jax.random.fold_in(key, list_salt))
    senders = jax.random.randint(source_key, (BUCKETS, width), 0, CORES)
    raw_slots = jax.random.randint(slot_key, (BUCKETS, width), 0, 1 << 20)
    chips = jnp.arange(BUCKETS, dtype=jnp.int32) // (BUCKETS // CHIPS)
    limits = counts[senders, chips[:, None]]
    return (senders * capacity + raw_slots % limits).astype(jnp.int32)


def draw_send_ids(key, part):
    return send_table(key, RQ, 11, 12)


def draw_near_list(key, part):
    return list_table(key, RQ, 11, 13, NEAR)


def draw_cell_send_ids(key, part):
    return send_table(key, RQC, 21, 22)


def draw_far_list(key, part):
    return list_table(key, RQC, 21, 23, FAR)


def draw_active(key, part):
    active_key = jax.random.fold_in(key, 31)
    count_key, spot_key, order_key = jax.random.split(active_key, 3)
    drawn = jax.random.randint(count_key, (CORES,), 0, ACT_MAX)
    counts = 1 + drawn * drawn // ACT_MAX
    busiest = jax.random.randint(spot_key, (), 0, CORES)
    counts = jnp.where(jnp.arange(CORES, dtype=jnp.int32) == busiest, ACT_MAX, counts)
    orders = jax.vmap(lambda order_seed: jax.random.permutation(order_seed, NB))(jax.random.split(order_key, CORES))
    return (orders < counts[:, None]).astype(jnp.int32).reshape(BUCKETS)


def draw_positions(key, part):
    center_key, offset_key = jax.random.split(jax.random.fold_in(key, 41))
    centers = jnp.clip(0.7 * jax.random.normal(center_key, (3, BUCKETS), jnp.float32), -4.0, 4.0)
    offsets = jnp.clip(0.5 * jax.random.normal(offset_key, (3, BUCKETS, BUCKET), jnp.float32), -2.0, 2.0)
    return (centers[:, :, None] + offsets).reshape(3, PARTICLES)


def plant(result, key, low, high):
    longest = result.shape.index(max(result.shape))
    spots = []
    for shift in (0, 1):
        where = [jax.random.randint(jax.random.fold_in(key, axis), (), 0, length) for axis, length in enumerate(result.shape)]
        where[longest] = (where[longest] + shift) % result.shape[longest]
        spots.append(tuple(where))
    return result.at[spots[0]].set(low).at[spots[1]].set(high)


def steps_of(key, shape, shards, least, high):
    factor_of, own = 1.0, jax.random.fold_in(key, 6)
    for dim, blocks in shards:
        steps = jnp.exp(jax.random.uniform(jax.random.fold_in(own, dim), (blocks,), jnp.float32, least / len(shards), high / len(shards)))
        factor_of = factor_of * jnp.repeat(steps, shape[dim] // blocks).reshape([-1 if axis == dim else 1 for axis in range(len(shape))])
    return factor_of


def noise(own_key, extent, spread, limit, cuts=(), kind=jnp.bfloat16):
    array = jax.random.normal(own_key, extent, jnp.float32) * spread
    if len(cuts) > 0:
        array = steps_of(own_key, extent, cuts, -0.22, 0.18) * array
    return jnp.clip(array, min=-limit, max=limit).astype(kind)


def setup_inputs(seed: int = 0) -> dict:
    arg_keys = jax.random.split(jax.random.key(seed), 12)
    return {
        "positions": draw_positions(jax.random.fold_in(arg_keys[11], 71), 0),
        "masses": jnp.clip(jnp.exp(math.log(0.005) - 2.30258502 * jax.random.uniform(arg_keys[1], (PARTICLES,), jnp.float32) ** steps_of(arg_keys[1], (PARTICLES,), ((0, 32),), -0.2, 0.2)), 0.0005, 0.005),
        "old_accel": noise(arg_keys[2], (3, PARTICLES), 1.0, 6.0, ((1, 32),), jnp.float32),
        "active": draw_active(jax.random.fold_in(arg_keys[11], 71), 0),
        "parent_of": plant(jax.random.randint(arg_keys[4], (BUCKETS,), 0, NPAR), jax.random.fold_in(arg_keys[4], 1), 0, NPAR - 1).astype(jnp.int32),
        "parent_centers": noise(arg_keys[5], (3, NPAR), 0.7, 4.0, (), jnp.float32),
        "local_list": plant(jax.random.randint(arg_keys[6], (BUCKETS, LOCAL_N), 0, 2 * NB), jax.random.fold_in(arg_keys[6], 1), 0, (2 * NB) - 1).astype(jnp.int32),
        "near_list": draw_near_list(jax.random.fold_in(arg_keys[11], 71), 0),
        "far_list": draw_far_list(jax.random.fold_in(arg_keys[11], 71), 0),
        "send_ids": draw_send_ids(jax.random.fold_in(arg_keys[11], 71), 0),
        "cell_send_ids": draw_cell_send_ids(jax.random.fold_in(arg_keys[11], 71), 0),
    }


soft_sq = 0.0025
far_sq = 0.25

def exponent_rows():
    listing = []
    for degree in range(5):
        for power_x in range(degree, -1, -1):
            for power_y in range(degree - power_x, -1, -1):
                listing.append((power_x, power_y, degree - power_x - power_y))
    return listing

def multinomial(triple):
    return math.factorial(sum(triple)) / (math.factorial(triple[0]) * math.factorial(triple[1]) * math.factorial(triple[2]))

def weight_layout():
    triples = exponent_rows()
    position = {triple: number for number, triple in enumerate(triples)}
    weight_table = np.zeros((46, 35))
    s_scale = [1.0, 1.0, 1.5, 2.5, 4.375]
    t_scale = [-0.5, -1.5, -3.75]
    mono_index = []
    radial_index = []
    for number, triple in enumerate(triples):
        weight_table[number, number] = multinomial(triple) * s_scale[sum(triple)]
        mono_index.append(number)
        radial_index.append(sum(triple))
    for number in range(10):
        triple = triples[number]
        for axis_at in range(3):
            raised = list(triple)
            raised[axis_at] += 2
            weight_table[35 + number, position[tuple(raised)]] += multinomial(triple) * t_scale[sum(triple)]
        mono_index.append(number)
        radial_index.append(sum(triple) + 1)
    for axis_one in range(3):
        for axis_two in range(3):
            raised = [0, 0, 0]
            raised[axis_one] += 2
            raised[axis_two] += 2
            weight_table[45, position[tuple(raised)]] += 0.375
    mono_index.append(0)
    radial_index.append(2)
    return (weight_table, mono_index, radial_index)

def monomial_list(comp_x, comp_y, comp_z):
    powers = []
    for component in (comp_x, comp_y, comp_z):
        series = [jnp.ones_like(component)]
        for degree in range(4):
            series.append(series[-1] * component)
        powers.append(series)
    return [powers[0][power_x] * powers[1][power_y] * powers[2][power_z] for power_x, power_y, power_z in exponent_rows()]

def moments_about(rows, centers):
    monomials = monomial_list(rows[:, 0] - centers[0][:, None], rows[:, 1] - centers[1][:, None], rows[:, 2] - centers[2][:, None])
    return jnp.stack([lax.optimization_barrier(jnp.sum(rows[:, 3] * monomial, axis=1)) for monomial in monomials])

def bucket_cells(rows):
    centers = lax.optimization_barrier(jnp.mean(rows[:, :3], axis=2)).T
    moments = moments_about(rows, centers)
    return jnp.concatenate([moments.T, centers.T], axis=1)

def near_field(targets, sources):

    def add_source(number, running):
        source = lax.dynamic_index_in_dim(sources, number, 0, keepdims=False)
        offset = source[:3, :, None] - targets[:, None, :]
        dist_sq = lax.optimization_barrier(jnp.sum(offset * offset, axis=0)) + soft_sq
        weight = source[3][:, None] / (dist_sq * jnp.sqrt(dist_sq))
        return running + lax.optimization_barrier(jnp.sum(offset * weight[None], axis=1))
    return lax.fori_loop(0, sources.shape[0], add_source, jnp.zeros(targets.shape, jnp.float32))

def far_field(targets, cells):
    weight_table, mono_index, radial_index = weight_layout()
    centers = cells[:, 35:38].T
    weights = jnp.dot(cells[:, :35], jnp.asarray(weight_table.T, dtype=jnp.float32), precision=lax.Precision.HIGHEST)

    def potential(points):
        offset = points[:, None, :] - centers[:, :, None]
        rho_sq = lax.optimization_barrier(jnp.sum(offset * offset, axis=0)) + far_sq
        inv_rho = 1.0 / jnp.sqrt(rho_sq)
        inv_sq = 1.0 / rho_sq
        radial = [inv_rho]
        for degree in range(4):
            radial.append(radial[-1] * inv_sq)
        monomials = monomial_list(offset[0], offset[1], offset[2])
        running = jnp.zeros(rho_sq.shape, jnp.float32)
        for number in range(46):
            running = running + monomials[mono_index[number]] * weights[:, number][:, None] * radial[radial_index[number]]
        return jnp.sum(running)
    return jax.grad(potential)(targets)

def reference(positions, masses, old_accel, active, parent_of, parent_centers, local_list, near_list, far_list, send_ids, cell_send_ids):
    rows = jnp.concatenate([positions, masses[None]], axis=0).reshape(4, BUCKETS, BUCKET).transpose(1, 0, 2)
    cells = bucket_cells(rows)
    parent_terms = moments_about(rows, parent_centers[:, parent_of])
    parent_moments = jax.ops.segment_sum(parent_terms.T, parent_of, num_segments=NPAR).T
    per_chip = BUCKETS // CHIPS
    bucket_ids = jnp.arange(BUCKETS, dtype=jnp.int32)
    chip_of = bucket_ids // per_chip
    local_global = (chip_of * per_chip)[:, None] + local_list
    near_device = near_list // RQ
    near_global = near_device * NB + send_ids[near_device, chip_of[:, None], near_list % RQ]
    far_device = far_list // RQC
    far_global = far_device * NB + cell_send_ids[far_device, chip_of[:, None], far_list % RQC]
    source_ids = jnp.concatenate([local_global, near_global], axis=1)

    def one_bucket(bucket_at):

        def compute(bucket_row):
            targets = rows[bucket_row, :3]
            return near_field(targets, rows[source_ids[bucket_row]]) + far_field(targets, cells[far_global[bucket_row]])

        def skipped(bucket_row):
            return jnp.zeros((3, BUCKET), jnp.float32)
        return lax.cond(active[bucket_at] > 0, compute, skipped, bucket_at)
    computed = lax.map(one_bucket, bucket_ids)
    new_accel = computed.transpose(1, 0, 2).reshape(3, PARTICLES)
    active_cols = jnp.repeat(active > 0, BUCKET)
    return (jnp.where(active_cols[None, :], new_accel, old_accel), parent_moments)
```

```python
import math

import jax
import jax.numpy as jnp
import numpy as np
from jax import lax
from jax.experimental import pallas as pl
from jax.experimental.pallas import tpu as pltpu
from jax.sharding import PartitionSpec as P

BUCKET = 256
NB = 32
RQ = 4
RQC = 8


soft_sq = 0.0025
far_sq = 0.25


def exponent_rows():
    listing = []
    for degree in range(5):
        for power_x in range(degree, -1, -1):
            for power_y in range(degree - power_x, -1, -1):
                listing.append((power_x, power_y, degree - power_x - power_y))
    return listing


def multinomial(triple):
    return math.factorial(sum(triple)) / (
        math.factorial(triple[0]) * math.factorial(triple[1]) * math.factorial(triple[2])
    )


def weight_layout():
    triples = exponent_rows()
    position = {triple: number for number, triple in enumerate(triples)}
    weight_table = np.zeros((46, 35))
    s_scale = [1.0, 1.0, 1.5, 2.5, 4.375]
    t_scale = [-0.5, -1.5, -3.75]
    mono_index = []
    radial_index = []
    for number, triple in enumerate(triples):
        weight_table[number, number] = multinomial(triple) * s_scale[sum(triple)]
        mono_index.append(number)
        radial_index.append(sum(triple))
    for number in range(10):
        triple = triples[number]
        for axis_at in range(3):
            raised = list(triple)
            raised[axis_at] += 2
            weight_table[35 + number, position[tuple(raised)]] += (
                multinomial(triple) * t_scale[sum(triple)]
            )
        mono_index.append(number)
        radial_index.append(sum(triple) + 1)
    for axis_one in range(3):
        for axis_two in range(3):
            raised = [0, 0, 0]
            raised[axis_one] += 2
            raised[axis_two] += 2
            weight_table[45, position[tuple(raised)]] += 0.375
    mono_index.append(0)
    radial_index.append(2)
    return (weight_table, mono_index, radial_index)


def monomial_list(comp_x, comp_y, comp_z):
    powers = []
    for component in (comp_x, comp_y, comp_z):
        series = [jnp.ones_like(component)]
        for degree in range(4):
            series.append(series[-1] * component)
        powers.append(series)
    return [
        powers[0][power_x] * powers[1][power_y] * powers[2][power_z]
        for power_x, power_y, power_z in exponent_rows()
    ]


def moments_about(rows, centers):
    monomials = monomial_list(
        rows[:, 0] - centers[0][:, None],
        rows[:, 1] - centers[1][:, None],
        rows[:, 2] - centers[2][:, None],
    )
    return jnp.stack([jnp.sum(rows[:, 3] * monomial, axis=1) for monomial in monomials])


def bucket_cells(rows):
    centers = jnp.mean(rows[:, :3], axis=2).T
    moments = moments_about(rows, centers)
    return jnp.concatenate([moments.T, centers.T], axis=1)


def gradient_table():
    weight_table, _, _ = weight_layout()
    triples = exponent_rows()
    position = {triple: number for number, triple in enumerate(triples)}
    table = np.zeros((128, 38))

    def lowered(numbers, first, base, start, count):
        for offset, number in enumerate(numbers):
            triple = triples[first + offset]
            for axis_at in range(3):
                if triple[axis_at] > 0:
                    less = list(triple)
                    less[axis_at] -= 1
                    column = base + axis_at * count + position[tuple(less)] - start
                    table[column, :35] += triple[axis_at] * weight_table[number]

    lowered(range(20, 35), 20, 0, 10, 10)
    lowered(range(10, 20), 10, 30, 4, 6)
    lowered(range(39, 45), 4, 48, 1, 3)
    lowered(range(4, 10), 4, 57, 1, 3)
    lowered(range(36, 39), 1, 66, 0, 1)
    lowered(range(1, 4), 1, 69, 0, 1)
    table[72, :35] = weight_table[0]
    table[73, :35] = weight_table[35]
    table[74, :35] = weight_table[45]
    for axis_at in range(3):
        table[75 + axis_at, 35 + axis_at] = 1.0
    return table


def split_three(value):
    first = value.astype(jnp.bfloat16).astype(jnp.float32)
    rest = value - first
    second = rest.astype(jnp.bfloat16).astype(jnp.float32)
    return first, second, rest - second


def weighted(columns, base, monomials):
    total = columns[base] * monomials[0]
    for number in range(1, len(monomials)):
        total = total + columns[base + number] * monomials[number]
    return total


def far_group(cells, points):
    columns = [cells[:, number : number + 1] for number in range(78)]
    r = [points[axis_at : axis_at + 1, :] - columns[75 + axis_at] for axis_at in range(3)]
    x, y, z = r
    xx, xy, xz, yy, yz, zz = x * x, x * y, x * z, y * y, y * z, z * z
    rho_sq = xx + yy + zz + far_sq
    inv_rho = lax.rsqrt(rho_sq)
    inv_sq = inv_rho * inv_rho
    radial = [inv_rho]
    for degree in range(5):
        radial.append(radial[-1] * inv_sq)
    quad = [xx, xy, xz, yy, yz, zz]
    cubic = [
        xx * x, xx * y, xx * z, x * yy, x * yz, x * zz, yy * y, yy * z, y * zz, zz * z,
    ]

    def dot(grad):
        return x * grad[0] + y * grad[1] + z * grad[2]

    grad_four = [weighted(columns, 10 * axis_at, cubic) for axis_at in range(3)]
    scalar = (2.25 * radial[5]) * dot(grad_four)
    total = [radial[4] * grad for grad in grad_four]
    grad_three = [weighted(columns, 30 + 6 * axis_at, quad) for axis_at in range(3)]
    grad_two_t = [weighted(columns, 48 + 3 * axis_at, r) for axis_at in range(3)]
    value_three = dot(grad_three) * (1.0 / 3.0) + dot(grad_two_t) * 0.5
    scalar = scalar + (7.0 * radial[4]) * value_three
    total = [
        t + radial[3] * (a + b) for t, a, b in zip(total, grad_three, grad_two_t)
    ]
    grad_two = [weighted(columns, 57 + 3 * axis_at, r) for axis_at in range(3)]
    value_two = dot(grad_two) * 0.5 + dot(columns[66:69]) + columns[74]
    scalar = scalar + (5.0 * radial[3]) * value_two
    total = [
        t + radial[2] * (a + b) for t, a, b in zip(total, grad_two, columns[66:69])
    ]
    value_one = dot(columns[69:72]) + columns[73]
    scalar = scalar + (3.0 * radial[2]) * value_one + radial[1] * columns[72]
    return [t + radial[1] * a - c * scalar for t, a, c in zip(total, columns[69:72], r)]


def field_kernel(
    active_ref, local_ref, near_ref, far_ref, chip_ref, pool_ref, cell_ref, old_ref, out_ref, cells
):
    my_sub = lax.axis_index("sub")
    out_ref[...] = old_ref[...]
    buckets = out_ref.shape[1] // BUCKET
    row_at = lax.broadcasted_iota(jnp.int32, (8, BUCKET), 0)

    def eight(value):
        return jnp.concatenate([value, jnp.zeros((4, BUCKET), jnp.float32)], axis=0)

    def visit(bucket, carry):
        row = my_sub * buckets + bucket

        @pl.when(active_ref[row] > 0)
        def _():
            target = eight(chip_ref[row])
            middle = jnp.mean(target, axis=1, keepdims=True)
            at = jnp.where(row_at < 3, target - middle, 0.0)
            norm = jnp.sum(at * at, axis=0, keepdims=True) + soft_sq
            feature = jnp.where(
                row_at == 3, 1.0, jnp.where(row_at == 4, norm, -2.0 * at)
            )
            one, two, three = split_three(feature)
            lhs = jnp.concatenate([one, two, one, two, three, one], axis=0).T.astype(jnp.bfloat16)
            running = jnp.zeros((24, BUCKET), jnp.float32)
            for number in range(local_ref.shape[1] + near_ref.shape[1]):
                if number < local_ref.shape[1]:
                    source = eight(chip_ref[local_ref[row, number]])
                else:
                    source = eight(pool_ref[near_ref[row, number - local_ref.shape[1]]])
                mass = source[3:4, :]
                offset = jnp.where(row_at < 3, source - middle, 0.0)
                size = jnp.sum(offset * offset, axis=0, keepdims=True)
                feature = jnp.where(
                    row_at == 3, size, jnp.where(row_at == 4, 1.0, offset)
                )
                one, two, three = split_three(feature)
                rhs = jnp.concatenate([one, one, two, two, one, three], axis=0).astype(jnp.bfloat16)
                carried = jnp.where(row_at == 3, 1.0, offset) * mass
                values = jnp.concatenate(split_three(carried), axis=0).astype(jnp.bfloat16)
                dist_sq = jnp.dot(lhs, rhs, preferred_element_type=jnp.float32)
                inv = lax.rsqrt(dist_sq)
                weight = inv * inv * inv
                coarse = weight.astype(jnp.bfloat16)
                fine = (weight - coarse.astype(jnp.float32)).astype(jnp.bfloat16)
                for part in (coarse, fine):
                    running = running + lax.dot_general(
                        values, part, (((1,), (1,)), ((), ())), preferred_element_type=jnp.float32
                    )
            summed = running[0:8] + running[8:16] + running[16:24]
            near = summed - at * summed[3:4, :]
            count = far_ref.shape[1]
            for number in range(count):
                cells[pl.ds(number, 1), :] = cell_ref[pl.ds(far_ref[row, number], 1), :]
            parts = None
            for group in range(count // 8):
                piece = far_group(cells[8 * group : 8 * group + 8, :], target)
                parts = piece if parts is None else [a + b for a, b in zip(parts, piece)]
            far = jnp.concatenate([jnp.sum(part, axis=0, keepdims=True) for part in parts], axis=0)
            out_ref[:, pl.ds(pl.multiple_of(bucket * BUCKET, BUCKET), BUCKET)] = near[0:3] + far

        return carry

    lax.fori_loop(0, buckets, visit, 0)


def fields(active, local_list, near_list, far_list, chip_rows, pool_rows, pool_table, old_accel):
    smem = pl.BlockSpec(memory_space=pltpu.SMEM)
    vmem = pl.BlockSpec(memory_space=pltpu.VMEM)
    return pl.pallas_call(
        field_kernel,
        out_shape=jax.ShapeDtypeStruct(old_accel.shape, jnp.float32),
        in_specs=[smem] * 4 + [vmem] * 4,
        out_specs=vmem,
        scratch_shapes=[pltpu.VMEM((far_list.shape[1], 128), jnp.float32)],
    )(active, local_list, near_list, far_list, chip_rows, pool_rows, pool_table, old_accel)


def pool_index(entries, slot_total, chip_count, sub_count):
    device = entries // slot_total
    return (
        device % sub_count * (chip_count * slot_total)
        + device // sub_count * slot_total
        + entries % slot_total
    )


def local(
    positions,
    masses,
    old_accel,
    active,
    parent_of,
    parent_centers,
    local_list,
    near_list,
    far_list,
    send_ids,
    cell_send_ids,
):
    sub_count = lax.axis_size("sub")
    chip_count = lax.axis_size("dom")
    own_rows = (
        jnp.concatenate([positions, masses[None]], axis=0).reshape(4, NB, BUCKET).transpose(1, 0, 2)
    )
    own_cells = jnp.dot(
        bucket_cells(own_rows),
        jnp.asarray(gradient_table().T, dtype=jnp.float32),
        precision=lax.Precision.HIGHEST,
    )
    parent_total = parent_centers.shape[1]
    one_hot = (parent_of[:, None] == jnp.arange(parent_total, dtype=jnp.int32)[None, :]).astype(
        jnp.float32
    )
    centers_of = lax.dot_general(
        parent_centers, one_hot, (((1,), (1,)), ((), ())), precision=lax.Precision.HIGHEST
    )
    contribution = jnp.dot(
        moments_about(own_rows, centers_of), one_hot, precision=lax.Precision.HIGHEST
    )
    chip_sum = lax.psum(contribution, "sub")
    parent_moments = lax.psum_scatter(chip_sum, "dom", scatter_dimension=1, tiled=True)
    bucket_pick = send_ids[0]
    blocks = jnp.where(
        (bucket_pick >= 0)[:, :, None, None], own_rows[jnp.maximum(bucket_pick, 0)], 0.0
    )
    cell_pick = cell_send_ids[0]
    cell_blocks = jnp.where((cell_pick >= 0)[:, :, None], own_cells[jnp.maximum(cell_pick, 0)], 0.0)
    chip_parts, chip_blocks, chip_cells = (
        lax.all_gather(own_rows[None], "sub", axis=0, tiled=True),
        lax.all_gather(blocks[None], "sub", axis=0, tiled=True),
        lax.all_gather(cell_blocks[None], "sub", axis=0, tiled=True),
    )
    pool_blocks, pool_cells = (
        lax.all_to_all(chip_blocks, "dom", split_axis=1, concat_axis=1, tiled=True),
        lax.all_to_all(chip_cells, "dom", split_axis=1, concat_axis=1, tiled=True),
    )
    chip_rows = chip_parts.reshape(sub_count * NB, 4, BUCKET)
    pool_rows = pool_blocks.reshape(sub_count * chip_count * RQ, 4, BUCKET)
    pool_table = pool_cells.reshape(sub_count * chip_count * RQC, 128)
    near_pool = pool_index(near_list, RQ, chip_count, sub_count)
    far_pool = pool_index(far_list, RQC, chip_count, sub_count)

    accel = fields(
        active, local_list, near_pool, far_pool, chip_rows, pool_rows, pool_table, old_accel
    )
    return (accel, parent_moments)


def solution(mesh):
    return jax.shard_map(
        local,
        mesh=mesh,
        in_specs=(
            P(None, ("dom", "sub")),
            P(("dom", "sub")),
            P(None, ("dom", "sub")),
            P("dom"),
            P(("dom", "sub")),
            P(),
            P("dom", None),
            P("dom", None),
            P("dom", None),
            P(("dom", "sub"), None, None),
            P(("dom", "sub"), None, None),
        ),
        out_specs=(P(None, ("dom", "sub")), P(None, "dom")),
        check_vma=False,
    )
```

```python
import math

import jax
import jax.numpy as jnp
import numpy as np
from jax import lax
from jax.experimental import pallas as pl
from jax.experimental.pallas import tpu as pltpu
from jax.sharding import PartitionSpec as P

BUCKET = 256
NB = 32
RQ = 4
RQC = 8


soft_sq = 0.0025
far_sq = 0.25


def exponent_rows():
    listing = []
    for degree in range(5):
        for power_x in range(degree, -1, -1):
            for power_y in range(degree - power_x, -1, -1):
                listing.append((power_x, power_y, degree - power_x - power_y))
    return listing


def multinomial(triple):
    return math.factorial(sum(triple)) / (
        math.factorial(triple[0]) * math.factorial(triple[1]) * math.factorial(triple[2])
    )


def weight_layout():
    triples = exponent_rows()
    position = {triple: number for number, triple in enumerate(triples)}
    weight_table = np.zeros((46, 35))
    s_scale = [1.0, 1.0, 1.5, 2.5, 4.375]
    t_scale = [-0.5, -1.5, -3.75]
    mono_index = []
    radial_index = []
    for number, triple in enumerate(triples):
        weight_table[number, number] = multinomial(triple) * s_scale[sum(triple)]
        mono_index.append(number)
        radial_index.append(sum(triple))
    for number in range(10):
        triple = triples[number]
        for axis_at in range(3):
            raised = list(triple)
            raised[axis_at] += 2
            weight_table[35 + number, position[tuple(raised)]] += (
                multinomial(triple) * t_scale[sum(triple)]
            )
        mono_index.append(number)
        radial_index.append(sum(triple) + 1)
    for axis_one in range(3):
        for axis_two in range(3):
            raised = [0, 0, 0]
            raised[axis_one] += 2
            raised[axis_two] += 2
            weight_table[45, position[tuple(raised)]] += 0.375
    mono_index.append(0)
    radial_index.append(2)
    return (weight_table, mono_index, radial_index)


def monomial_list(comp_x, comp_y, comp_z):
    powers = []
    for component in (comp_x, comp_y, comp_z):
        series = [jnp.ones_like(component)]
        for degree in range(4):
            series.append(series[-1] * component)
        powers.append(series)
    return [
        powers[0][power_x] * powers[1][power_y] * powers[2][power_z]
        for power_x, power_y, power_z in exponent_rows()
    ]


def moments_about(rows, centers):
    monomials = monomial_list(
        rows[:, 0] - centers[0][:, None],
        rows[:, 1] - centers[1][:, None],
        rows[:, 2] - centers[2][:, None],
    )
    return jnp.stack([jnp.sum(rows[:, 3] * monomial, axis=1) for monomial in monomials])


def bucket_cells(rows):
    centers = jnp.mean(rows[:, :3], axis=2).T
    moments = moments_about(rows, centers)
    return jnp.concatenate([moments.T, centers.T], axis=1)


def gradient_table():
    weight_table, _, _ = weight_layout()
    triples = exponent_rows()
    position = {triple: number for number, triple in enumerate(triples)}
    table = np.zeros((128, 38))

    def lowered(numbers, first, base, start, count):
        for offset, number in enumerate(numbers):
            triple = triples[first + offset]
            for axis_at in range(3):
                if triple[axis_at] > 0:
                    less = list(triple)
                    less[axis_at] -= 1
                    column = base + axis_at * count + position[tuple(less)] - start
                    table[column, :35] += triple[axis_at] * weight_table[number]

    lowered(range(20, 35), 20, 0, 10, 10)
    lowered(range(10, 20), 10, 30, 4, 6)
    lowered(range(39, 45), 4, 48, 1, 3)
    lowered(range(4, 10), 4, 57, 1, 3)
    lowered(range(36, 39), 1, 66, 0, 1)
    lowered(range(1, 4), 1, 69, 0, 1)
    table[72, :35] = weight_table[0]
    table[73, :35] = weight_table[35]
    table[74, :35] = weight_table[45]
    for axis_at in range(3):
        table[75 + axis_at, 35 + axis_at] = 1.0
    return table


def split_three(value):
    first = value.astype(jnp.bfloat16).astype(jnp.float32)
    rest = value - first
    second = rest.astype(jnp.bfloat16).astype(jnp.float32)
    return first, second, rest - second


def weighted(columns, base, monomials):
    total = columns[base] * monomials[0]
    for number in range(1, len(monomials)):
        total = total + columns[base + number] * monomials[number]
    return total


def far_group(cells, points):
    columns = [cells[:, number : number + 1] for number in range(78)]
    r = [points[axis_at : axis_at + 1, :] - columns[75 + axis_at] for axis_at in range(3)]
    x, y, z = r
    xx, xy, xz, yy, yz, zz = x * x, x * y, x * z, y * y, y * z, z * z
    rho_sq = xx + yy + zz + far_sq
    inv_rho = lax.rsqrt(rho_sq)
    inv_sq = inv_rho * inv_rho
    radial = [inv_rho]
    for degree in range(5):
        radial.append(radial[-1] * inv_sq)
    quad = [xx, xy, xz, yy, yz, zz]
    cubic = [
        xx * x, xx * y, xx * z, x * yy, x * yz, x * zz, yy * y, yy * z, y * zz, zz * z,
    ]

    def dot(grad):
        return x * grad[0] + y * grad[1] + z * grad[2]

    grad_four = [weighted(columns, 10 * axis_at, cubic) for axis_at in range(3)]
    scalar = (2.25 * radial[5]) * dot(grad_four)
    total = [radial[4] * grad for grad in grad_four]
    grad_three = [weighted(columns, 30 + 6 * axis_at, quad) for axis_at in range(3)]
    grad_two_t = [weighted(columns, 48 + 3 * axis_at, r) for axis_at in range(3)]
    value_three = dot(grad_three) * (1.0 / 3.0) + dot(grad_two_t) * 0.5
    scalar = scalar + (7.0 * radial[4]) * value_three
    total = [
        t + radial[3] * (a + b) for t, a, b in zip(total, grad_three, grad_two_t)
    ]
    grad_two = [weighted(columns, 57 + 3 * axis_at, r) for axis_at in range(3)]
    value_two = dot(grad_two) * 0.5 + dot(columns[66:69]) + columns[74]
    scalar = scalar + (5.0 * radial[3]) * value_two
    total = [
        t + radial[2] * (a + b) for t, a, b in zip(total, grad_two, columns[66:69])
    ]
    value_one = dot(columns[69:72]) + columns[73]
    scalar = scalar + (3.0 * radial[2]) * value_one + radial[1] * columns[72]
    return [t + radial[1] * a - c * scalar for t, a, c in zip(total, columns[69:72], r)]


def field_kernel(
    active_ref, local_ref, near_ref, far_ref, chip_ref, pool_ref, cell_ref, old_ref, out_ref, cells
):
    my_sub = lax.axis_index("sub")
    out_ref[...] = old_ref[...]
    buckets = out_ref.shape[1] // BUCKET
    row_at = lax.broadcasted_iota(jnp.int32, (8, BUCKET), 0)

    def eight(value):
        return jnp.concatenate([value, jnp.zeros((4, BUCKET), jnp.float32)], axis=0)

    def visit(bucket, carry):
        row = my_sub * buckets + bucket

        @pl.when(active_ref[row] > 0)
        def _():
            target = eight(chip_ref[row])
            middle = jnp.mean(target, axis=1, keepdims=True)
            at = jnp.where(row_at < 3, target - middle, 0.0)
            norm = jnp.sum(at * at, axis=0, keepdims=True) + soft_sq
            feature = jnp.where(
                row_at == 3, 1.0, jnp.where(row_at == 4, norm, -2.0 * at)
            )
            one, two, three = split_three(feature)
            lhs = jnp.concatenate([one, two, one, two, three, one], axis=0).T.astype(jnp.bfloat16)
            running = jnp.zeros((24, BUCKET), jnp.float32)
            for number in range(local_ref.shape[1] + near_ref.shape[1]):
                if number < local_ref.shape[1]:
                    source = eight(chip_ref[local_ref[row, number]])
                else:
                    source = eight(pool_ref[near_ref[row, number - local_ref.shape[1]]])
                mass = source[3:4, :]
                offset = jnp.where(row_at < 3, source - middle, 0.0)
                size = jnp.sum(offset * offset, axis=0, keepdims=True)
                feature = jnp.where(
                    row_at == 3, size, jnp.where(row_at == 4, 1.0, offset)
                )
                one, two, three = split_three(feature)
                rhs = jnp.concatenate([one, one, two, two, one, three], axis=0).astype(jnp.bfloat16)
                carried = jnp.where(row_at == 3, 1.0, offset) * mass
                values = jnp.concatenate(split_three(carried), axis=0).astype(jnp.bfloat16)
                dist_sq = jnp.dot(lhs, rhs, preferred_element_type=jnp.float32)
                inv = lax.rsqrt(dist_sq)
                weight = inv * inv * inv
                coarse = weight.astype(jnp.bfloat16)
                fine = (weight - coarse.astype(jnp.float32)).astype(jnp.bfloat16)
                for part in (coarse, fine):
                    running = running + lax.dot_general(
                        values, part, (((1,), (1,)), ((), ())), preferred_element_type=jnp.float32
                    )
            summed = running[0:8] + running[8:16] + running[16:24]
            near = summed - at * summed[3:4, :]
            count = far_ref.shape[1]
            for number in range(count):
                cells[pl.ds(number, 1), :] = cell_ref[pl.ds(far_ref[row, number], 1), :]
            parts = None
            for group in range(count // 8):
                piece = far_group(cells[8 * group : 8 * group + 8, :], target)
                parts = piece if parts is None else [a + b for a, b in zip(parts, piece)]
            far = jnp.concatenate([jnp.sum(part, axis=0, keepdims=True) for part in parts], axis=0)
            out_ref[:, pl.ds(pl.multiple_of(bucket * BUCKET, BUCKET), BUCKET)] = near[0:3] + far

        return carry

    lax.fori_loop(0, buckets, visit, 0)


def fields(active, local_list, near_list, far_list, chip_rows, pool_rows, pool_table, old_accel):
    smem = pl.BlockSpec(memory_space=pltpu.SMEM)
    vmem = pl.BlockSpec(memory_space=pltpu.VMEM)
    return pl.pallas_call(
        field_kernel,
        out_shape=jax.ShapeDtypeStruct(old_accel.shape, jnp.float32),
        in_specs=[smem] * 4 + [vmem] * 4,
        out_specs=vmem,
        scratch_shapes=[pltpu.VMEM((far_list.shape[1], 128), jnp.float32)],
    )(active, local_list, near_list, far_list, chip_rows, pool_rows, pool_table, old_accel)


def exchange_kernel(
    rows_ref, blocks_ref, cells_ref, terms_ref,
    chip_ref, pool_ref, table_ref, parent_ref,
    parts, send_sem, recv_sem,
):
    subs = lax.axis_size("sub")
    devices = lax.axis_size("dom") * subs
    my_dom = lax.axis_index("dom")
    my_sub = lax.axis_index("sub")
    me = my_dom * subs + my_sub
    count = rows_ref.shape[0]
    barrier = pltpu.get_barrier_semaphore()

    def coordinates(step):
        other = lax.rem(me + step, devices)
        return other // subs, lax.rem(other, subs)

    def greet(step, carry):
        pl.semaphore_signal(
            barrier, inc=1, device_id=coordinates(step), device_id_type=pl.DeviceIdType.MESH
        )
        return carry

    lax.fori_loop(1, devices, greet, 0)
    pl.semaphore_wait(barrier, devices - 1)
    outgoing = ((blocks_ref, pool_ref), (cells_ref, table_ref), (terms_ref, parts))
    own_rows = chip_ref.at[pl.ds(my_sub * count, count)]

    for step in range(1, subs):
        pltpu.make_async_remote_copy(
            src_ref=rows_ref,
            dst_ref=own_rows,
            send_sem=send_sem.at[3],
            recv_sem=recv_sem.at[3],
            device_id=(my_dom, lax.rem(my_sub + step, subs)),
            device_id_type=pl.DeviceIdType.MESH,
        ).start()

    def send(step, carry):
        to_dom, to_sub = coordinates(step)
        for number, (source, sink) in enumerate(outgoing):
            pltpu.make_async_remote_copy(
                src_ref=source.at[to_dom],
                dst_ref=sink.at[me],
                send_sem=send_sem.at[number],
                recv_sem=recv_sem.at[number],
                device_id=(to_dom, to_sub),
                device_id_type=pl.DeviceIdType.MESH,
            ).start()
        return carry

    lax.fori_loop(1, devices, send, 0)
    for number, (source, sink) in enumerate(outgoing):
        pltpu.make_async_copy(source.at[my_dom], sink.at[me], recv_sem.at[number]).start()
    pltpu.make_async_copy(rows_ref, own_rows, recv_sem.at[3]).start()
    for number, (source, sink) in enumerate(outgoing):
        sent = sink.at[pl.ds(0, devices - 1)]
        pltpu.make_async_copy(sent, sent, send_sem.at[number]).wait()
        pltpu.make_async_copy(sink, sink, recv_sem.at[number]).wait()
    sent = chip_ref.at[pl.ds(0, count * (subs - 1))]
    pltpu.make_async_copy(sent, sent, send_sem.at[3]).wait()
    pltpu.make_async_copy(chip_ref, chip_ref, recv_sem.at[3]).wait()
    total = jnp.sum(parts[...], axis=0)
    parent_ref[...] = total.T[: parent_ref.shape[0], :]


def exchange(rows, blocks, cells, terms, moment_count):
    subs = lax.axis_size("sub")
    devices = lax.axis_size("dom") * subs
    vmem = pl.BlockSpec(memory_space=pltpu.VMEM)
    shapes = (
        (rows.shape[0] * subs,) + rows.shape[1:],
        (devices,) + blocks.shape[1:],
        (devices,) + cells.shape[1:],
        (moment_count, terms.shape[1]),
    )
    return pl.pallas_call(
        exchange_kernel,
        out_shape=[jax.ShapeDtypeStruct(shape, jnp.float32) for shape in shapes],
        in_specs=[vmem] * 4,
        out_specs=[vmem] * 4,
        scratch_shapes=[
            pltpu.VMEM((devices,) + terms.shape[1:], jnp.float32),
            pltpu.SemaphoreType.DMA((4,)),
            pltpu.SemaphoreType.DMA((4,)),
        ],
        compiler_params=pltpu.CompilerParams(collective_id=0, has_side_effects=True),
    )(rows, blocks, cells, terms)


def local(
    positions,
    masses,
    old_accel,
    active,
    parent_of,
    parent_centers,
    local_list,
    near_list,
    far_list,
    send_ids,
    cell_send_ids,
):
    chip_count = lax.axis_size("dom")
    own_rows = (
        jnp.concatenate([positions, masses[None]], axis=0).reshape(4, NB, BUCKET).transpose(1, 0, 2)
    )
    own_cells = jnp.dot(
        bucket_cells(own_rows),
        jnp.asarray(gradient_table().T, dtype=jnp.float32),
        precision=lax.Precision.HIGHEST,
    )
    parent_total = parent_centers.shape[1]
    one_hot = (parent_of[:, None] == jnp.arange(parent_total, dtype=jnp.int32)[None, :]).astype(
        jnp.float32
    )
    centers_of = lax.dot_general(
        parent_centers, one_hot, (((1,), (1,)), ((), ())), precision=lax.Precision.HIGHEST
    )
    terms = moments_about(own_rows, centers_of)
    moment_count = terms.shape[0]
    contribution = lax.dot_general(
        one_hot,
        jnp.pad(terms, ((0, 128 - moment_count), (0, 0))),
        (((0,), (1,)), ((), ())),
        precision=lax.Precision.HIGHEST,
    ).reshape(chip_count, parent_total // chip_count, 128)
    blocks = own_rows[jnp.maximum(send_ids[0], 0)]
    cell_blocks = own_cells[jnp.maximum(cell_send_ids[0], 0)]
    chip_rows, pool_blocks, pool_cells, parent_moments = exchange(
        own_rows, blocks, cell_blocks, contribution, moment_count
    )
    pool_rows = pool_blocks.reshape(-1, 4, BUCKET)
    pool_table = pool_cells.reshape(-1, 128)
    accel = fields(
        active, local_list, near_list, far_list, chip_rows, pool_rows, pool_table, old_accel
    )
    return (accel, parent_moments)


def solution(mesh):
    return jax.shard_map(
        local,
        mesh=mesh,
        in_specs=(
            P(None, ("dom", "sub")),
            P(("dom", "sub")),
            P(None, ("dom", "sub")),
            P("dom"),
            P(("dom", "sub")),
            P(),
            P("dom", None),
            P("dom", None),
            P("dom", None),
            P(("dom", "sub"), None, None),
            P(("dom", "sub"), None, None),
        ),
        out_specs=(P(None, ("dom", "sub")), P(None, "dom")),
        check_vma=False,
    )
```

```python
import math

import jax
import jax.numpy as jnp
import numpy as np
from jax import lax
from jax.experimental import pallas as pl
from jax.experimental.pallas import tpu as pltpu
from jax.sharding import PartitionSpec as P

BUCKET = 256
NB = 32
RQ = 4
RQC = 8


soft_sq = 0.0025
far_sq = 0.25


def exponent_rows():
    listing = []
    for degree in range(5):
        for power_x in range(degree, -1, -1):
            for power_y in range(degree - power_x, -1, -1):
                listing.append((power_x, power_y, degree - power_x - power_y))
    return listing


def multinomial(triple):
    return math.factorial(sum(triple)) / (
        math.factorial(triple[0]) * math.factorial(triple[1]) * math.factorial(triple[2])
    )


def weight_layout():
    triples = exponent_rows()
    position = {triple: number for number, triple in enumerate(triples)}
    weight_table = np.zeros((46, 35))
    s_scale = [1.0, 1.0, 1.5, 2.5, 4.375]
    t_scale = [-0.5, -1.5, -3.75]
    mono_index = []
    radial_index = []
    for number, triple in enumerate(triples):
        weight_table[number, number] = multinomial(triple) * s_scale[sum(triple)]
        mono_index.append(number)
        radial_index.append(sum(triple))
    for number in range(10):
        triple = triples[number]
        for axis_at in range(3):
            raised = list(triple)
            raised[axis_at] += 2
            weight_table[35 + number, position[tuple(raised)]] += (
                multinomial(triple) * t_scale[sum(triple)]
            )
        mono_index.append(number)
        radial_index.append(sum(triple) + 1)
    for axis_one in range(3):
        for axis_two in range(3):
            raised = [0, 0, 0]
            raised[axis_one] += 2
            raised[axis_two] += 2
            weight_table[45, position[tuple(raised)]] += 0.375
    mono_index.append(0)
    radial_index.append(2)
    return (weight_table, mono_index, radial_index)


def monomial_list(comp_x, comp_y, comp_z):
    powers = []
    for component in (comp_x, comp_y, comp_z):
        series = [jnp.ones_like(component)]
        for degree in range(4):
            series.append(series[-1] * component)
        powers.append(series)
    return [
        powers[0][power_x] * powers[1][power_y] * powers[2][power_z]
        for power_x, power_y, power_z in exponent_rows()
    ]


def moments_about(rows, centers):
    monomials = monomial_list(
        rows[:, 0] - centers[0][:, None],
        rows[:, 1] - centers[1][:, None],
        rows[:, 2] - centers[2][:, None],
    )
    return jnp.stack([jnp.sum(rows[:, 3] * monomial, axis=1) for monomial in monomials])


def bucket_cells(rows):
    centers = jnp.mean(rows[:, :3], axis=2).T
    moments = moments_about(rows, centers)
    return jnp.concatenate([moments.T, centers.T], axis=1)


def gradient_table():
    weight_table, _, _ = weight_layout()
    triples = exponent_rows()
    position = {triple: number for number, triple in enumerate(triples)}
    table = np.zeros((128, 38))

    def lowered(numbers, first, base, start, count):
        for offset, number in enumerate(numbers):
            triple = triples[first + offset]
            for axis_at in range(3):
                if triple[axis_at] > 0:
                    less = list(triple)
                    less[axis_at] -= 1
                    column = base + axis_at * count + position[tuple(less)] - start
                    table[column, :35] += triple[axis_at] * weight_table[number]

    lowered(range(20, 35), 20, 0, 10, 10)
    lowered(range(10, 20), 10, 30, 4, 6)
    lowered(range(39, 45), 4, 48, 1, 3)
    lowered(range(4, 10), 4, 57, 1, 3)
    lowered(range(36, 39), 1, 66, 0, 1)
    lowered(range(1, 4), 1, 69, 0, 1)
    table[72, :35] = weight_table[0]
    table[73, :35] = weight_table[35]
    table[74, :35] = weight_table[45]
    for axis_at in range(3):
        table[75 + axis_at, 35 + axis_at] = 1.0
    return table


def split_three(value):
    first = value.astype(jnp.bfloat16).astype(jnp.float32)
    rest = value - first
    second = rest.astype(jnp.bfloat16).astype(jnp.float32)
    return first, second, rest - second


def weighted(columns, base, monomials):
    total = columns[base] * monomials[0]
    for number in range(1, len(monomials)):
        total = total + columns[base + number] * monomials[number]
    return total


def far_group(cells, points):
    columns = [cells[:, number : number + 1] for number in range(78)]
    r = [points[axis_at : axis_at + 1, :] - columns[75 + axis_at] for axis_at in range(3)]
    x, y, z = r
    xx, xy, xz, yy, yz, zz = x * x, x * y, x * z, y * y, y * z, z * z
    rho_sq = xx + yy + zz + far_sq
    inv_rho = lax.rsqrt(rho_sq)
    inv_sq = inv_rho * inv_rho
    radial = [inv_rho]
    for degree in range(5):
        radial.append(radial[-1] * inv_sq)
    quad = [xx, xy, xz, yy, yz, zz]
    cubic = [
        xx * x, xx * y, xx * z, x * yy, x * yz, x * zz, yy * y, yy * z, y * zz, zz * z,
    ]

    def dot(grad):
        return x * grad[0] + y * grad[1] + z * grad[2]

    grad_four = [weighted(columns, 10 * axis_at, cubic) for axis_at in range(3)]
    scalar = (2.25 * radial[5]) * dot(grad_four)
    total = [radial[4] * grad for grad in grad_four]
    grad_three = [weighted(columns, 30 + 6 * axis_at, quad) for axis_at in range(3)]
    grad_two_t = [weighted(columns, 48 + 3 * axis_at, r) for axis_at in range(3)]
    value_three = dot(grad_three) * (1.0 / 3.0) + dot(grad_two_t) * 0.5
    scalar = scalar + (7.0 * radial[4]) * value_three
    total = [
        t + radial[3] * (a + b) for t, a, b in zip(total, grad_three, grad_two_t)
    ]
    grad_two = [weighted(columns, 57 + 3 * axis_at, r) for axis_at in range(3)]
    value_two = dot(grad_two) * 0.5 + dot(columns[66:69]) + columns[74]
    scalar = scalar + (5.0 * radial[3]) * value_two
    total = [
        t + radial[2] * (a + b) for t, a, b in zip(total, grad_two, columns[66:69])
    ]
    value_one = dot(columns[69:72]) + columns[73]
    scalar = scalar + (3.0 * radial[2]) * value_one + radial[1] * columns[72]
    return [t + radial[1] * a - c * scalar for t, a, c in zip(total, columns[69:72], r)]


def field_kernel(
    active_ref, local_ref, near_ref, far_ref, chip_ref, pool_ref, cell_ref, old_ref, out_ref, cells
):
    my_sub = lax.axis_index("sub")
    out_ref[...] = old_ref[...]
    buckets = out_ref.shape[1] // BUCKET
    row_at = lax.broadcasted_iota(jnp.int32, (8, BUCKET), 0)

    def eight(value):
        return jnp.concatenate([value, jnp.zeros((4, BUCKET), jnp.float32)], axis=0)

    def visit(bucket, carry):
        row = my_sub * buckets + bucket

        @pl.when(active_ref[row] > 0)
        def _():
            target = eight(chip_ref[row])
            middle = jnp.mean(target, axis=1, keepdims=True)
            at = jnp.where(row_at < 3, target - middle, 0.0)
            norm = jnp.sum(at * at, axis=0, keepdims=True) + soft_sq
            feature = jnp.where(
                row_at == 3, 1.0, jnp.where(row_at == 4, norm, -2.0 * at)
            )
            one, two, three = split_three(feature)
            lhs = jnp.concatenate([one, two, one, two, three, one], axis=0).astype(jnp.bfloat16)
            running = jnp.zeros((24, BUCKET), jnp.float32)
            for number in range(local_ref.shape[0] + near_ref.shape[0]):
                if number < local_ref.shape[0]:
                    source = eight(chip_ref[local_ref[number, row]])
                else:
                    source = eight(pool_ref[near_ref[number - local_ref.shape[0], row]])
                mass = source[3:4, :]
                offset = jnp.where(row_at < 3, source - middle, 0.0)
                size = jnp.sum(offset * offset, axis=0, keepdims=True)
                feature = jnp.where(
                    row_at == 3, size, jnp.where(row_at == 4, 1.0, offset)
                )
                one, two, three = split_three(feature)
                rhs = jnp.concatenate([one, one, two, two, one, three], axis=0).T.astype(jnp.bfloat16)
                carried = jnp.where(row_at == 3, 1.0, offset) * mass
                values = jnp.concatenate(split_three(carried), axis=0).astype(jnp.bfloat16)
                dist_sq = jnp.dot(rhs, lhs, preferred_element_type=jnp.float32)
                inv = lax.rsqrt(dist_sq)
                weight = inv * inv * inv
                coarse = weight.astype(jnp.bfloat16)
                fine = (weight - coarse.astype(jnp.float32)).astype(jnp.bfloat16)
                for part in (coarse, fine):
                    running = running + lax.dot_general(
                        values, part, (((1,), (0,)), ((), ())), preferred_element_type=jnp.float32
                    )
            summed = running[0:8] + running[8:16] + running[16:24]
            near = summed - at * summed[3:4, :]
            count = far_ref.shape[0]
            for number in range(count):
                cells[pl.ds(number, 1), :] = cell_ref[pl.ds(far_ref[number, row], 1), :]
            parts = None
            for group in range(count // 8):
                piece = far_group(cells[8 * group : 8 * group + 8, :], target)
                parts = piece if parts is None else [a + b for a, b in zip(parts, piece)]
            far = jnp.concatenate([jnp.sum(part, axis=0, keepdims=True) for part in parts], axis=0)
            out_ref[:, pl.ds(pl.multiple_of(bucket * BUCKET, BUCKET), BUCKET)] = near[0:3] + far

        return carry

    lax.fori_loop(0, buckets, visit, 0)


def fields(active, local_list, near_list, far_list, chip_rows, pool_rows, pool_table, old_accel):
    smem = pl.BlockSpec(memory_space=pltpu.SMEM)
    vmem = pl.BlockSpec(memory_space=pltpu.VMEM)
    return pl.pallas_call(
        field_kernel,
        out_shape=jax.ShapeDtypeStruct(old_accel.shape, jnp.float32),
        in_specs=[smem] * 4 + [vmem] * 4,
        out_specs=vmem,
        scratch_shapes=[pltpu.VMEM((far_list.shape[1], 128), jnp.float32)],
    )(active, local_list.T, near_list.T, far_list.T, chip_rows, pool_rows, pool_table, old_accel)


def exchange_kernel(
    rows_ref, blocks_ref, cells_ref, terms_ref,
    chip_ref, pool_ref, table_ref, parent_ref,
    parts, send_sem, recv_sem,
):
    subs = lax.axis_size("sub")
    devices = lax.axis_size("dom") * subs
    my_dom = lax.axis_index("dom")
    my_sub = lax.axis_index("sub")
    me = my_dom * subs + my_sub
    count = rows_ref.shape[0]
    barrier = pltpu.get_barrier_semaphore()

    def coordinates(step):
        other = lax.rem(me + step, devices)
        return other // subs, lax.rem(other, subs)

    def greet(step, carry):
        pl.semaphore_signal(
            barrier, inc=1, device_id=coordinates(step), device_id_type=pl.DeviceIdType.MESH
        )
        return carry

    lax.fori_loop(1, devices, greet, 0)
    pl.semaphore_wait(barrier, devices - 1)
    outgoing = ((blocks_ref, pool_ref), (cells_ref, table_ref), (terms_ref, parts))
    own_rows = chip_ref.at[pl.ds(my_sub * count, count)]

    for step in range(1, subs):
        pltpu.make_async_remote_copy(
            src_ref=rows_ref,
            dst_ref=own_rows,
            send_sem=send_sem.at[3],
            recv_sem=recv_sem.at[3],
            device_id=(my_dom, lax.rem(my_sub + step, subs)),
            device_id_type=pl.DeviceIdType.MESH,
        ).start()

    def send(step, carry):
        to_dom, to_sub = coordinates(step)
        for number, (source, sink) in enumerate(outgoing):
            pltpu.make_async_remote_copy(
                src_ref=source.at[to_dom],
                dst_ref=sink.at[me],
                send_sem=send_sem.at[number],
                recv_sem=recv_sem.at[number],
                device_id=(to_dom, to_sub),
                device_id_type=pl.DeviceIdType.MESH,
            ).start()
        return carry

    lax.fori_loop(1, devices, send, 0)
    for number, (source, sink) in enumerate(outgoing):
        pltpu.make_async_copy(source.at[my_dom], sink.at[me], recv_sem.at[number]).start()
    pltpu.make_async_copy(rows_ref, own_rows, recv_sem.at[3]).start()
    for number, (source, sink) in enumerate(outgoing):
        sent = sink.at[pl.ds(0, devices - 1)]
        pltpu.make_async_copy(sent, sent, send_sem.at[number]).wait()
        pltpu.make_async_copy(sink, sink, recv_sem.at[number]).wait()
    sent = chip_ref.at[pl.ds(0, count * (subs - 1))]
    pltpu.make_async_copy(sent, sent, send_sem.at[3]).wait()
    pltpu.make_async_copy(chip_ref, chip_ref, recv_sem.at[3]).wait()
    total = jnp.sum(parts[...], axis=0)
    parent_ref[...] = total.T[: parent_ref.shape[0], :]


def exchange(rows, blocks, cells, terms, moment_count):
    subs = lax.axis_size("sub")
    devices = lax.axis_size("dom") * subs
    vmem = pl.BlockSpec(memory_space=pltpu.VMEM)
    shapes = (
        (rows.shape[0] * subs,) + rows.shape[1:],
        (devices,) + blocks.shape[1:],
        (devices,) + cells.shape[1:],
        (moment_count, terms.shape[1]),
    )
    return pl.pallas_call(
        exchange_kernel,
        out_shape=[jax.ShapeDtypeStruct(shape, jnp.float32) for shape in shapes],
        in_specs=[vmem] * 4,
        out_specs=[vmem] * 4,
        scratch_shapes=[
            pltpu.VMEM((devices,) + terms.shape[1:], jnp.float32),
            pltpu.SemaphoreType.DMA((4,)),
            pltpu.SemaphoreType.DMA((4,)),
        ],
        compiler_params=pltpu.CompilerParams(collective_id=0, has_side_effects=True),
    )(rows, blocks, cells, terms)


def local(
    positions,
    masses,
    old_accel,
    active,
    parent_of,
    parent_centers,
    local_list,
    near_list,
    far_list,
    send_ids,
    cell_send_ids,
):
    chip_count = lax.axis_size("dom")
    own_rows = (
        jnp.concatenate([positions, masses[None]], axis=0).reshape(4, NB, BUCKET).transpose(1, 0, 2)
    )
    own_cells = jnp.dot(
        bucket_cells(own_rows),
        jnp.asarray(gradient_table().T, dtype=jnp.float32),
        precision=lax.Precision.HIGHEST,
    )
    parent_total = parent_centers.shape[1]
    one_hot = (parent_of[:, None] == jnp.arange(parent_total, dtype=jnp.int32)[None, :]).astype(
        jnp.float32
    )
    centers_of = lax.dot_general(
        parent_centers, one_hot, (((1,), (1,)), ((), ())), precision=lax.Precision.HIGHEST
    )
    terms = moments_about(own_rows, centers_of)
    moment_count = terms.shape[0]
    contribution = lax.dot_general(
        one_hot,
        jnp.pad(terms, ((0, 128 - moment_count), (0, 0))),
        (((0,), (1,)), ((), ())),
        precision=lax.Precision.HIGHEST,
    ).reshape(chip_count, parent_total // chip_count, 128)
    blocks = own_rows[jnp.maximum(send_ids[0], 0)]
    cell_blocks = own_cells[jnp.maximum(cell_send_ids[0], 0)]
    chip_rows, pool_blocks, pool_cells, parent_moments = exchange(
        own_rows, blocks, cell_blocks, contribution, moment_count
    )
    pool_rows = pool_blocks.reshape(-1, 4, BUCKET)
    pool_table = pool_cells.reshape(-1, 128)
    accel = fields(
        active, local_list, near_list, far_list, chip_rows, pool_rows, pool_table, old_accel
    )
    return (accel, parent_moments)


def solution(mesh):
    return jax.shard_map(
        local,
        mesh=mesh,
        in_specs=(
            P(None, ("dom", "sub")),
            P(("dom", "sub")),
            P(None, ("dom", "sub")),
            P("dom"),
            P(("dom", "sub")),
            P(),
            P("dom", None),
            P("dom", None),
            P("dom", None),
            P(("dom", "sub"), None, None),
            P(("dom", "sub"), None, None),
        ),
        out_specs=(P(None, ("dom", "sub")), P(None, "dom")),
        check_vma=False,
    )
```

```python
import math

import jax
import jax.numpy as jnp
import numpy as np
from jax import lax
from jax.experimental import pallas as pl
from jax.experimental.pallas import tpu as pltpu
from jax.sharding import PartitionSpec as P

BUCKET = 256
NB = 32
RQ = 4
RQC = 8


soft_sq = 0.0025
far_sq = 0.25


def exponent_rows():
    listing = []
    for degree in range(5):
        for power_x in range(degree, -1, -1):
            for power_y in range(degree - power_x, -1, -1):
                listing.append((power_x, power_y, degree - power_x - power_y))
    return listing


def multinomial(triple):
    return math.factorial(sum(triple)) / (
        math.factorial(triple[0]) * math.factorial(triple[1]) * math.factorial(triple[2])
    )


def weight_layout():
    triples = exponent_rows()
    position = {triple: number for number, triple in enumerate(triples)}
    weight_table = np.zeros((46, 35))
    s_scale = [1.0, 1.0, 1.5, 2.5, 4.375]
    t_scale = [-0.5, -1.5, -3.75]
    mono_index = []
    radial_index = []
    for number, triple in enumerate(triples):
        weight_table[number, number] = multinomial(triple) * s_scale[sum(triple)]
        mono_index.append(number)
        radial_index.append(sum(triple))
    for number in range(10):
        triple = triples[number]
        for axis_at in range(3):
            raised = list(triple)
            raised[axis_at] += 2
            weight_table[35 + number, position[tuple(raised)]] += (
                multinomial(triple) * t_scale[sum(triple)]
            )
        mono_index.append(number)
        radial_index.append(sum(triple) + 1)
    for axis_one in range(3):
        for axis_two in range(3):
            raised = [0, 0, 0]
            raised[axis_one] += 2
            raised[axis_two] += 2
            weight_table[45, position[tuple(raised)]] += 0.375
    mono_index.append(0)
    radial_index.append(2)
    return (weight_table, mono_index, radial_index)


def monomial_list(comp_x, comp_y, comp_z):
    powers = []
    for component in (comp_x, comp_y, comp_z):
        series = [jnp.ones_like(component)]
        for degree in range(4):
            series.append(series[-1] * component)
        powers.append(series)
    return [
        powers[0][power_x] * powers[1][power_y] * powers[2][power_z]
        for power_x, power_y, power_z in exponent_rows()
    ]


def moments_about(rows, centers):
    monomials = monomial_list(
        rows[:, 0] - centers[0][:, None],
        rows[:, 1] - centers[1][:, None],
        rows[:, 2] - centers[2][:, None],
    )
    return jnp.stack([jnp.sum(rows[:, 3] * monomial, axis=1) for monomial in monomials])


def bucket_cells(rows):
    centers = jnp.mean(rows[:, :3], axis=2).T
    moments = moments_about(rows, centers)
    return jnp.concatenate([moments.T, centers.T], axis=1)


def gradient_table():
    weight_table, _, _ = weight_layout()
    triples = exponent_rows()
    position = {triple: number for number, triple in enumerate(triples)}
    table = np.zeros((128, 38))

    def lowered(numbers, first, base, start, count):
        for offset, number in enumerate(numbers):
            triple = triples[first + offset]
            for axis_at in range(3):
                if triple[axis_at] > 0:
                    less = list(triple)
                    less[axis_at] -= 1
                    column = base + axis_at * count + position[tuple(less)] - start
                    table[column, :35] += triple[axis_at] * weight_table[number]

    lowered(range(20, 35), 20, 0, 10, 10)
    lowered(range(10, 20), 10, 30, 4, 6)
    lowered(range(39, 45), 4, 48, 1, 3)
    lowered(range(4, 10), 4, 57, 1, 3)
    lowered(range(36, 39), 1, 66, 0, 1)
    lowered(range(1, 4), 1, 69, 0, 1)
    table[72, :35] = weight_table[0]
    table[73, :35] = weight_table[35]
    table[74, :35] = weight_table[45]
    for axis_at in range(3):
        table[75 + axis_at, 35 + axis_at] = 1.0
    return table


def split_three(value):
    first = value.astype(jnp.bfloat16).astype(jnp.float32)
    rest = value - first
    second = rest.astype(jnp.bfloat16).astype(jnp.float32)
    return first, second, rest - second


def weighted(columns, base, monomials):
    total = columns[base] * monomials[0]
    for number in range(1, len(monomials)):
        total = total + columns[base + number] * monomials[number]
    return total


def far_group(cells, points):
    columns = [cells[:, number : number + 1] for number in range(78)]
    r = [points[axis_at : axis_at + 1, :] - columns[75 + axis_at] for axis_at in range(3)]
    x, y, z = r
    xx, xy, xz, yy, yz, zz = x * x, x * y, x * z, y * y, y * z, z * z
    rho_sq = xx + yy + zz + far_sq
    inv_rho = lax.rsqrt(rho_sq)
    inv_sq = inv_rho * inv_rho
    radial = [inv_rho]
    for degree in range(5):
        radial.append(radial[-1] * inv_sq)
    quad = [xx, xy, xz, yy, yz, zz]
    cubic = [
        xx * x, xx * y, xx * z, x * yy, x * yz, x * zz, yy * y, yy * z, y * zz, zz * z,
    ]

    def dot(grad):
        return x * grad[0] + y * grad[1] + z * grad[2]

    grad_four = [weighted(columns, 10 * axis_at, cubic) for axis_at in range(3)]
    scalar = (2.25 * radial[5]) * dot(grad_four)
    total = [radial[4] * grad for grad in grad_four]
    grad_three = [weighted(columns, 30 + 6 * axis_at, quad) for axis_at in range(3)]
    grad_two_t = [weighted(columns, 48 + 3 * axis_at, r) for axis_at in range(3)]
    value_three = dot(grad_three) * (1.0 / 3.0) + dot(grad_two_t) * 0.5
    scalar = scalar + (7.0 * radial[4]) * value_three
    total = [
        t + radial[3] * (a + b) for t, a, b in zip(total, grad_three, grad_two_t)
    ]
    grad_two = [weighted(columns, 57 + 3 * axis_at, r) for axis_at in range(3)]
    value_two = dot(grad_two) * 0.5 + dot(columns[66:69]) + columns[74]
    scalar = scalar + (5.0 * radial[3]) * value_two
    total = [
        t + radial[2] * (a + b) for t, a, b in zip(total, grad_two, columns[66:69])
    ]
    value_one = dot(columns[69:72]) + columns[73]
    scalar = scalar + (3.0 * radial[2]) * value_one + radial[1] * columns[72]
    return [t + radial[1] * a - c * scalar for t, a, c in zip(total, columns[69:72], r)]


def field_kernel(
    active_ref, local_ref, near_ref, far_ref, chip_ref, pool_ref, cell_ref, old_ref, out_ref, cells
):
    my_sub = lax.axis_index("sub")
    out_ref[...] = old_ref[...]
    buckets = out_ref.shape[1] // BUCKET
    row_at = lax.broadcasted_iota(jnp.int32, (8, BUCKET), 0)

    subs, chips = lax.axis_size("sub"), lax.axis_size("dom")

    def slot(entry, slots):
        device = lax.div(entry, slots)
        place = lax.rem(device, subs) * chips + lax.div(device, subs)
        return place * slots + lax.rem(entry, slots)

    def eight(value):
        return jnp.concatenate([value, jnp.zeros((4, BUCKET), jnp.float32)], axis=0)

    def visit(bucket, carry):
        row = my_sub * buckets + bucket

        @pl.when(active_ref[row] > 0)
        def _():
            target = eight(chip_ref[row])
            middle = jnp.mean(target, axis=1, keepdims=True)
            at = jnp.where(row_at < 3, target - middle, 0.0)
            norm = jnp.sum(at * at, axis=0, keepdims=True) + soft_sq
            feature = jnp.where(
                row_at == 3, 1.0, jnp.where(row_at == 4, norm, -2.0 * at)
            )
            one, two, three = split_three(feature)
            lhs = jnp.concatenate([one, two, one, two, three, one], axis=0).astype(jnp.bfloat16)
            running = jnp.zeros((24, BUCKET), jnp.float32)
            for number in range(local_ref.shape[0] + near_ref.shape[0]):
                if number < local_ref.shape[0]:
                    source = eight(chip_ref[local_ref[number, row]])
                else:
                    source = eight(pool_ref[slot(near_ref[number - local_ref.shape[0], row], RQ)])
                mass = source[3:4, :]
                offset = jnp.where(row_at < 3, source - middle, 0.0)
                size = jnp.sum(offset * offset, axis=0, keepdims=True)
                feature = jnp.where(
                    row_at == 3, size, jnp.where(row_at == 4, 1.0, offset)
                )
                one, two, three = split_three(feature)
                rhs = jnp.concatenate([one, one, two, two, one, three], axis=0).T.astype(jnp.bfloat16)
                carried = jnp.where(row_at == 3, 1.0, offset) * mass
                values = jnp.concatenate(split_three(carried), axis=0).astype(jnp.bfloat16)
                dist_sq = jnp.dot(rhs, lhs, preferred_element_type=jnp.float32)
                inv = lax.rsqrt(dist_sq)
                weight = inv * inv * inv
                coarse = weight.astype(jnp.bfloat16)
                fine = (weight - coarse.astype(jnp.float32)).astype(jnp.bfloat16)
                for part in (coarse, fine):
                    running = running + lax.dot_general(
                        values, part, (((1,), (0,)), ((), ())), preferred_element_type=jnp.float32
                    )
            summed = running[0:8] + running[8:16] + running[16:24]
            near = summed - at * summed[3:4, :]
            count = far_ref.shape[0]
            for number in range(count):
                cells[pl.ds(number, 1), :] = cell_ref[pl.ds(slot(far_ref[number, row], RQC), 1), :]
            parts = None
            for group in range(count // 8):
                piece = far_group(cells[8 * group : 8 * group + 8, :], target)
                parts = piece if parts is None else [a + b for a, b in zip(parts, piece)]
            far = jnp.concatenate([jnp.sum(part, axis=0, keepdims=True) for part in parts], axis=0)
            out_ref[:, pl.ds(pl.multiple_of(bucket * BUCKET, BUCKET), BUCKET)] = near[0:3] + far

        return carry

    lax.fori_loop(0, buckets, visit, 0)


def fields(active, local_list, near_list, far_list, chip_rows, pool_rows, pool_table, old_accel):
    smem = pl.BlockSpec(memory_space=pltpu.SMEM)
    vmem = pl.BlockSpec(memory_space=pltpu.VMEM)
    return pl.pallas_call(
        field_kernel,
        out_shape=jax.ShapeDtypeStruct(old_accel.shape, jnp.float32),
        in_specs=[smem] * 4 + [vmem] * 4,
        out_specs=vmem,
        scratch_shapes=[pltpu.VMEM((far_list.shape[1], 128), jnp.float32)],
    )(active, local_list.T, near_list.T, far_list.T, chip_rows, pool_rows, pool_table, old_accel)


def exchange_kernel(
    rows_ref, blocks_ref, cells_ref, terms_ref,
    chip_ref, pool_ref, table_ref, parent_ref,
    parts, send_sem, recv_sem,
):
    subs = lax.axis_size("sub")
    my_dom = lax.axis_index("dom")
    my_sub = lax.axis_index("sub")
    chips = lax.axis_size("dom")
    count = rows_ref.shape[0]
    barrier = pltpu.get_barrier_semaphore()
    mesh_ids = pl.DeviceIdType.MESH

    def chip_at(step):
        return lax.rem(my_dom + step, chips)

    def greet(step, carry):
        pl.semaphore_signal(
            barrier, inc=1, device_id=(chip_at(step), my_sub), device_id_type=mesh_ids
        )
        return carry

    lax.fori_loop(1, chips, greet, 0)
    siblings = [(my_dom, lax.rem(my_sub + step, subs)) for step in range(1, subs)]
    for sibling in siblings:
        pl.semaphore_signal(barrier, inc=1, device_id=sibling, device_id_type=mesh_ids)
    pl.semaphore_wait(barrier, chips + subs - 2)
    outgoing = ((terms_ref, parts), (cells_ref, table_ref), (blocks_ref, pool_ref))
    own_rows = chip_ref.at[pl.ds(my_sub * count, count)]

    def send(step, carry):
        to_dom = chip_at(step)
        for number, (source, sink) in enumerate(outgoing):
            pltpu.make_async_remote_copy(
                src_ref=source.at[to_dom],
                dst_ref=sink.at[my_sub, my_dom],
                send_sem=send_sem.at[number],
                recv_sem=recv_sem.at[number],
                device_id=(to_dom, my_sub),
                device_id_type=mesh_ids,
            ).start()
        return carry

    lax.fori_loop(1, chips, send, 0)
    for sibling in siblings:
        pltpu.make_async_remote_copy(
            src_ref=rows_ref,
            dst_ref=own_rows,
            send_sem=send_sem.at[3],
            recv_sem=recv_sem.at[3],
            device_id=sibling,
            device_id_type=mesh_ids,
        ).start()
    for number, (source, sink) in enumerate(outgoing):
        pltpu.make_async_copy(
            source.at[my_dom], sink.at[my_sub, my_dom], recv_sem.at[number]
        ).start()
    pltpu.make_async_copy(rows_ref, own_rows, recv_sem.at[3]).start()
    for number, (source, sink) in enumerate(outgoing):
        half = sink.at[my_sub]
        pltpu.make_async_copy(half, half, recv_sem.at[number]).wait()
        for sibling in siblings:
            pltpu.make_async_remote_copy(
                src_ref=half,
                dst_ref=half,
                send_sem=send_sem.at[4 + number],
                recv_sem=recv_sem.at[4 + number],
                device_id=sibling,
                device_id_type=mesh_ids,
            ).start()
    for number, (source, sink) in enumerate(outgoing):
        sent = sink.at[0, pl.ds(0, chips - 1)]
        pltpu.make_async_copy(sent, sent, send_sem.at[number]).wait()
        others = sink.at[pl.ds(0, subs - 1)]
        pltpu.make_async_copy(others, others, send_sem.at[4 + number]).wait()
        pltpu.make_async_copy(others, others, recv_sem.at[4 + number]).wait()
    sent = chip_ref.at[pl.ds(0, count * (subs - 1))]
    pltpu.make_async_copy(sent, sent, send_sem.at[3]).wait()
    pltpu.make_async_copy(chip_ref, chip_ref, recv_sem.at[3]).wait()
    total = jnp.sum(parts[...], axis=(0, 1))
    parent_ref[...] = total.T[: parent_ref.shape[0], :]


def exchange(rows, blocks, cells, terms, moment_count):
    subs = lax.axis_size("sub")
    chips = lax.axis_size("dom")
    vmem = pl.BlockSpec(memory_space=pltpu.VMEM)
    shapes = (
        (rows.shape[0] * subs,) + rows.shape[1:],
        (subs, chips) + blocks.shape[1:],
        (subs, chips) + cells.shape[1:],
        (moment_count, terms.shape[1]),
    )
    return pl.pallas_call(
        exchange_kernel,
        out_shape=[jax.ShapeDtypeStruct(shape, jnp.float32) for shape in shapes],
        in_specs=[vmem] * 4,
        out_specs=[vmem] * 4,
        scratch_shapes=[
            pltpu.VMEM((subs, chips) + terms.shape[1:], jnp.float32),
            pltpu.SemaphoreType.DMA((7,)),
            pltpu.SemaphoreType.DMA((7,)),
        ],
        compiler_params=pltpu.CompilerParams(collective_id=0, has_side_effects=True),
    )(rows, blocks, cells, terms)


def local(
    positions,
    masses,
    old_accel,
    active,
    parent_of,
    parent_centers,
    local_list,
    near_list,
    far_list,
    send_ids,
    cell_send_ids,
):
    chip_count = lax.axis_size("dom")
    own_rows = (
        jnp.concatenate([positions, masses[None]], axis=0).reshape(4, NB, BUCKET).transpose(1, 0, 2)
    )
    own_cells = jnp.dot(
        bucket_cells(own_rows),
        jnp.asarray(gradient_table().T, dtype=jnp.float32),
        precision=lax.Precision.HIGHEST,
    )
    parent_total = parent_centers.shape[1]
    one_hot = (parent_of[:, None] == jnp.arange(parent_total, dtype=jnp.int32)[None, :]).astype(
        jnp.float32
    )
    centers_of = lax.dot_general(
        parent_centers, one_hot, (((1,), (1,)), ((), ())), precision=lax.Precision.HIGHEST
    )
    terms = moments_about(own_rows, centers_of)
    moment_count = terms.shape[0]
    contribution = lax.dot_general(
        one_hot,
        jnp.pad(terms, ((0, 128 - moment_count), (0, 0))),
        (((0,), (1,)), ((), ())),
        precision=lax.Precision.HIGHEST,
    ).reshape(chip_count, parent_total // chip_count, 128)
    blocks = own_rows.at[send_ids[0]].get(mode="clip")
    cell_blocks = own_cells.at[cell_send_ids[0]].get(mode="clip")
    chip_rows, pool_blocks, pool_cells, parent_moments = exchange(
        own_rows, blocks, cell_blocks, contribution, moment_count
    )
    pool_rows = pool_blocks.reshape(-1, 4, BUCKET)
    pool_table = pool_cells.reshape(-1, 128)
    accel = fields(
        active, local_list, near_list, far_list, chip_rows, pool_rows, pool_table, old_accel
    )
    return (accel, parent_moments)


def solution(mesh):
    return jax.shard_map(
        local,
        mesh=mesh,
        in_specs=(
            P(None, ("dom", "sub")),
            P(("dom", "sub")),
            P(None, ("dom", "sub")),
            P("dom"),
            P(("dom", "sub")),
            P(),
            P("dom", None),
            P("dom", None),
            P("dom", None),
            P(("dom", "sub"), None, None),
            P(("dom", "sub"), None, None),
        ),
        out_specs=(P(None, ("dom", "sub")), P(None, "dom")),
        check_vma=False,
    )
```

```python
import math

import jax
import jax.numpy as jnp
import numpy as np
from jax import lax
from jax.experimental import pallas as pl
from jax.experimental.pallas import tpu as pltpu
from jax.sharding import PartitionSpec as P

BUCKET = 256
NB = 32
RQ = 4
RQC = 8


soft_sq = 0.0025
far_sq = 0.25


def exponent_rows():
    listing = []
    for degree in range(5):
        for power_x in range(degree, -1, -1):
            for power_y in range(degree - power_x, -1, -1):
                listing.append((power_x, power_y, degree - power_x - power_y))
    return listing


def multinomial(triple):
    return math.factorial(sum(triple)) / (
        math.factorial(triple[0]) * math.factorial(triple[1]) * math.factorial(triple[2])
    )


def weight_layout():
    triples = exponent_rows()
    position = {triple: number for number, triple in enumerate(triples)}
    weight_table = np.zeros((46, 35))
    s_scale = [1.0, 1.0, 1.5, 2.5, 4.375]
    t_scale = [-0.5, -1.5, -3.75]
    mono_index = []
    radial_index = []
    for number, triple in enumerate(triples):
        weight_table[number, number] = multinomial(triple) * s_scale[sum(triple)]
        mono_index.append(number)
        radial_index.append(sum(triple))
    for number in range(10):
        triple = triples[number]
        for axis_at in range(3):
            raised = list(triple)
            raised[axis_at] += 2
            weight_table[35 + number, position[tuple(raised)]] += (
                multinomial(triple) * t_scale[sum(triple)]
            )
        mono_index.append(number)
        radial_index.append(sum(triple) + 1)
    for axis_one in range(3):
        for axis_two in range(3):
            raised = [0, 0, 0]
            raised[axis_one] += 2
            raised[axis_two] += 2
            weight_table[45, position[tuple(raised)]] += 0.375
    mono_index.append(0)
    radial_index.append(2)
    return (weight_table, mono_index, radial_index)


def monomial_list(comp_x, comp_y, comp_z):
    powers = []
    for component in (comp_x, comp_y, comp_z):
        series = [jnp.ones_like(component)]
        for degree in range(4):
            series.append(series[-1] * component)
        powers.append(series)
    return [
        powers[0][power_x] * powers[1][power_y] * powers[2][power_z]
        for power_x, power_y, power_z in exponent_rows()
    ]


def moments_about(rows, centers):
    monomials = monomial_list(
        rows[:, 0] - centers[0][:, None],
        rows[:, 1] - centers[1][:, None],
        rows[:, 2] - centers[2][:, None],
    )
    return jnp.stack([jnp.sum(rows[:, 3] * monomial, axis=1) for monomial in monomials])


def bucket_cells(rows):
    centers = jnp.mean(rows[:, :3], axis=2).T
    moments = moments_about(rows, centers)
    return jnp.concatenate([moments.T, centers.T], axis=1)


def gradient_table():
    weight_table, _, _ = weight_layout()
    triples = exponent_rows()
    position = {triple: number for number, triple in enumerate(triples)}
    table = np.zeros((128, 38))

    def lowered(numbers, first, base, start, count):
        for offset, number in enumerate(numbers):
            triple = triples[first + offset]
            for axis_at in range(3):
                if triple[axis_at] > 0:
                    less = list(triple)
                    less[axis_at] -= 1
                    column = base + axis_at * count + position[tuple(less)] - start
                    table[column, :35] += triple[axis_at] * weight_table[number]

    lowered(range(20, 35), 20, 0, 10, 10)
    lowered(range(10, 20), 10, 30, 4, 6)
    lowered(range(39, 45), 4, 48, 1, 3)
    lowered(range(4, 10), 4, 57, 1, 3)
    lowered(range(36, 39), 1, 66, 0, 1)
    lowered(range(1, 4), 1, 69, 0, 1)
    table[72, :35] = weight_table[0]
    table[73, :35] = weight_table[35]
    table[74, :35] = weight_table[45]
    for axis_at in range(3):
        table[75 + axis_at, 35 + axis_at] = 1.0
    return table


def split_three(value):
    first = value.astype(jnp.bfloat16).astype(jnp.float32)
    rest = value - first
    second = rest.astype(jnp.bfloat16).astype(jnp.float32)
    return first, second, rest - second


def weighted(columns, base, monomials):
    total = columns[base] * monomials[0]
    for number in range(1, len(monomials)):
        total = total + columns[base + number] * monomials[number]
    return total


def far_group(cells, points):
    columns = [cells[:, number : number + 1] for number in range(78)]
    r = [points[axis_at : axis_at + 1, :] - columns[75 + axis_at] for axis_at in range(3)]
    x, y, z = r
    xx, xy, xz, yy, yz, zz = x * x, x * y, x * z, y * y, y * z, z * z
    rho_sq = xx + yy + zz + far_sq
    inv_rho = lax.rsqrt(rho_sq)
    inv_sq = inv_rho * inv_rho
    radial = [inv_rho]
    for degree in range(5):
        radial.append(radial[-1] * inv_sq)
    quad = [xx, xy, xz, yy, yz, zz]
    cubic = [
        xx * x, xx * y, xx * z, x * yy, x * yz, x * zz, yy * y, yy * z, y * zz, zz * z,
    ]

    def dot(grad):
        return x * grad[0] + y * grad[1] + z * grad[2]

    grad_four = [weighted(columns, 10 * axis_at, cubic) for axis_at in range(3)]
    scalar = (2.25 * radial[5]) * dot(grad_four)
    total = [radial[4] * grad for grad in grad_four]
    grad_three = [weighted(columns, 30 + 6 * axis_at, quad) for axis_at in range(3)]
    grad_two_t = [weighted(columns, 48 + 3 * axis_at, r) for axis_at in range(3)]
    value_three = dot(grad_three) * (1.0 / 3.0) + dot(grad_two_t) * 0.5
    scalar = scalar + (7.0 * radial[4]) * value_three
    total = [
        t + radial[3] * (a + b) for t, a, b in zip(total, grad_three, grad_two_t)
    ]
    grad_two = [weighted(columns, 57 + 3 * axis_at, r) for axis_at in range(3)]
    value_two = dot(grad_two) * 0.5 + dot(columns[66:69]) + columns[74]
    scalar = scalar + (5.0 * radial[3]) * value_two
    total = [
        t + radial[2] * (a + b) for t, a, b in zip(total, grad_two, columns[66:69])
    ]
    value_one = dot(columns[69:72]) + columns[73]
    scalar = scalar + (3.0 * radial[2]) * value_one + radial[1] * columns[72]
    return [t + radial[1] * a - c * scalar for t, a, c in zip(total, columns[69:72], r)]


def field_kernel(
    active_ref, local_ref, near_ref, far_ref, chip_ref, pool_ref, cell_ref, old_ref, out_ref, cells
):
    my_sub = lax.axis_index("sub")
    out_ref[...] = old_ref[...]
    buckets = out_ref.shape[1] // BUCKET
    row_at = lax.broadcasted_iota(jnp.int32, (8, BUCKET), 0)

    subs, chips = lax.axis_size("sub"), lax.axis_size("dom")

    def slot(entry, slots):
        device = lax.div(entry, slots)
        place = lax.rem(device, subs) * chips + lax.div(device, subs)
        return place * slots + lax.rem(entry, slots)

    def eight(value):
        return jnp.concatenate([value, jnp.zeros((4, BUCKET), jnp.float32)], axis=0)

    def visit(bucket, carry):
        row = my_sub * buckets + bucket

        @pl.when(active_ref[row] > 0)
        def _():
            target = eight(chip_ref[row])
            middle = jnp.mean(target, axis=1, keepdims=True)
            at = jnp.where(row_at < 3, target - middle, 0.0)
            norm = jnp.sum(at * at, axis=0, keepdims=True) + soft_sq
            feature = jnp.where(
                row_at == 3, 1.0, jnp.where(row_at == 4, norm, -2.0 * at)
            )
            one, two, three = split_three(feature)
            lhs = jnp.concatenate([one, two, one, two, three, one], axis=0).astype(jnp.bfloat16)
            running = jnp.zeros((24, BUCKET), jnp.float32)
            for number in range(local_ref.shape[0] + near_ref.shape[0]):
                if number < local_ref.shape[0]:
                    source = eight(chip_ref[local_ref[number, row]])
                else:
                    source = eight(pool_ref[slot(near_ref[number - local_ref.shape[0], row], RQ)])
                mass = source[3:4, :]
                offset = jnp.where(row_at < 3, source - middle, 0.0)
                size = jnp.sum(offset * offset, axis=0, keepdims=True)
                feature = jnp.where(
                    row_at == 3, size, jnp.where(row_at == 4, 1.0, offset)
                )
                one, two, three = split_three(feature)
                rhs = jnp.concatenate([one, one, two, two, one, three], axis=0).T.astype(jnp.bfloat16)
                carried = jnp.where(row_at == 3, 1.0, offset) * mass
                values = jnp.concatenate(split_three(carried), axis=0).astype(jnp.bfloat16)
                dist_sq = jnp.dot(rhs, lhs, preferred_element_type=jnp.float32)
                inv = lax.rsqrt(dist_sq)
                weight = inv * inv * inv
                coarse = weight.astype(jnp.bfloat16)
                fine = (weight - coarse.astype(jnp.float32)).astype(jnp.bfloat16)
                for part in (coarse, fine):
                    running = running + lax.dot_general(
                        values, part, (((1,), (0,)), ((), ())), preferred_element_type=jnp.float32
                    )
            summed = running[0:8] + running[8:16] + running[16:24]
            near = summed - at * summed[3:4, :]
            count = far_ref.shape[0]
            for number in range(count):
                cells[pl.ds(number, 1), :] = cell_ref[pl.ds(slot(far_ref[number, row], RQC), 1), :]
            parts = None
            for group in range(count // 8):
                piece = far_group(cells[8 * group : 8 * group + 8, :], target)
                parts = piece if parts is None else [a + b for a, b in zip(parts, piece)]
            far = jnp.concatenate([jnp.sum(part, axis=0, keepdims=True) for part in parts], axis=0)
            out_ref[:, pl.ds(pl.multiple_of(bucket * BUCKET, BUCKET), BUCKET)] = near[0:3] + far

        return carry

    lax.fori_loop(0, buckets, visit, 0)


def fields(active, local_list, near_list, far_list, chip_rows, pool_rows, pool_table, old_accel):
    smem = pl.BlockSpec(memory_space=pltpu.SMEM)
    vmem = pl.BlockSpec(memory_space=pltpu.VMEM)
    return pl.pallas_call(
        field_kernel,
        out_shape=jax.ShapeDtypeStruct(old_accel.shape, jnp.float32),
        in_specs=[smem] * 4 + [vmem] * 4,
        out_specs=vmem,
        scratch_shapes=[pltpu.VMEM((far_list.shape[1], 128), jnp.float32)],
    )(active, local_list.T, near_list.T, far_list.T, chip_rows, pool_rows, pool_table, old_accel)


def exchange_kernel(
    rows_ref, blocks_ref, cells_ref, terms_ref,
    chip_ref, pool_ref, table_ref, parent_ref,
    parts, send_sem, recv_sem,
):
    subs = lax.axis_size("sub")
    my_dom = lax.axis_index("dom")
    my_sub = lax.axis_index("sub")
    chips = lax.axis_size("dom")
    count = rows_ref.shape[0]
    barrier = pltpu.get_barrier_semaphore()
    mesh_ids = pl.DeviceIdType.MESH

    def chip_at(step):
        return lax.rem(my_dom + step, chips)

    def greet(step, carry):
        pl.semaphore_signal(
            barrier, inc=1, device_id=(chip_at(step), my_sub), device_id_type=mesh_ids
        )
        return carry

    lax.fori_loop(1, chips, greet, 0)
    siblings = [(my_dom, lax.rem(my_sub + step, subs)) for step in range(1, subs)]
    for sibling in siblings:
        pl.semaphore_signal(barrier, inc=1, device_id=sibling, device_id_type=mesh_ids)
    pl.semaphore_wait(barrier, chips + subs - 2)
    outgoing = ((terms_ref, parts), (cells_ref, table_ref), (blocks_ref, pool_ref))
    own_rows = chip_ref.at[pl.ds(my_sub * count, count)]

    def send(step, carry):
        to_dom = chip_at(step)
        for number, (source, sink) in enumerate(outgoing):
            pltpu.make_async_remote_copy(
                src_ref=source.at[to_dom],
                dst_ref=sink.at[my_sub, my_dom],
                send_sem=send_sem.at[number],
                recv_sem=recv_sem.at[number],
                device_id=(to_dom, my_sub),
                device_id_type=mesh_ids,
            ).start()
        return carry

    lax.fori_loop(1, chips, send, 0)
    for sibling in siblings:
        pltpu.make_async_remote_copy(
            src_ref=rows_ref,
            dst_ref=own_rows,
            send_sem=send_sem.at[3],
            recv_sem=recv_sem.at[3],
            device_id=sibling,
            device_id_type=mesh_ids,
        ).start()
    for number, (source, sink) in enumerate(outgoing):
        pltpu.make_async_copy(
            source.at[my_dom], sink.at[my_sub, my_dom], recv_sem.at[number]
        ).start()
    pltpu.make_async_copy(rows_ref, own_rows, recv_sem.at[3]).start()
    for number, (source, sink) in enumerate(outgoing):
        half = sink.at[my_sub]
        pltpu.make_async_copy(half, half, recv_sem.at[number]).wait()
        for sibling in siblings:
            pltpu.make_async_remote_copy(
                src_ref=half,
                dst_ref=half,
                send_sem=send_sem.at[4 + number],
                recv_sem=recv_sem.at[4 + number],
                device_id=sibling,
                device_id_type=mesh_ids,
            ).start()
    for number, (source, sink) in enumerate(outgoing):
        sent = sink.at[0, pl.ds(0, chips - 1)]
        pltpu.make_async_copy(sent, sent, send_sem.at[number]).wait()
        others = sink.at[pl.ds(0, subs - 1)]
        pltpu.make_async_copy(others, others, send_sem.at[4 + number]).wait()
        pltpu.make_async_copy(others, others, recv_sem.at[4 + number]).wait()
    sent = chip_ref.at[pl.ds(0, count * (subs - 1))]
    pltpu.make_async_copy(sent, sent, send_sem.at[3]).wait()
    pltpu.make_async_copy(chip_ref, chip_ref, recv_sem.at[3]).wait()
    total = jnp.sum(parts[...], axis=(0, 1))
    parent_ref[...] = total[:, : parent_ref.shape[1]]


def exchange(rows, blocks, cells, terms, moment_count):
    subs = lax.axis_size("sub")
    chips = lax.axis_size("dom")
    vmem = pl.BlockSpec(memory_space=pltpu.VMEM)
    shapes = (
        (rows.shape[0] * subs,) + rows.shape[1:],
        (subs, chips) + blocks.shape[1:],
        (subs, chips) + cells.shape[1:],
        (terms.shape[1], moment_count),
    )
    return pl.pallas_call(
        exchange_kernel,
        out_shape=[jax.ShapeDtypeStruct(shape, jnp.float32) for shape in shapes],
        in_specs=[vmem] * 4,
        out_specs=[vmem] * 4,
        scratch_shapes=[
            pltpu.VMEM((subs, chips) + terms.shape[1:], jnp.float32),
            pltpu.SemaphoreType.DMA((7,)),
            pltpu.SemaphoreType.DMA((7,)),
        ],
        compiler_params=pltpu.CompilerParams(collective_id=0, has_side_effects=True),
    )(rows, blocks, cells, terms)


def local(
    positions,
    masses,
    old_accel,
    active,
    parent_of,
    parent_centers,
    local_list,
    near_list,
    far_list,
    send_ids,
    cell_send_ids,
):
    chip_count = lax.axis_size("dom")
    own_rows = (
        jnp.concatenate([positions, masses[None]], axis=0).reshape(4, NB, BUCKET).transpose(1, 0, 2)
    )
    own_cells = jnp.dot(
        bucket_cells(own_rows),
        jnp.asarray(gradient_table().T, dtype=jnp.float32),
        precision=lax.Precision.HIGHEST,
    )
    parent_total = parent_centers.shape[1]
    one_hot = (parent_of[:, None] == jnp.arange(parent_total, dtype=jnp.int32)[None, :]).astype(
        jnp.float32
    )
    centers_of = lax.dot_general(
        parent_centers, one_hot, (((1,), (1,)), ((), ())), precision=lax.Precision.HIGHEST
    )
    terms = moments_about(own_rows, centers_of)
    moment_count = terms.shape[0]
    contribution = lax.dot_general(
        one_hot,
        jnp.pad(terms, ((0, 128 - moment_count), (0, 0))),
        (((0,), (1,)), ((), ())),
        precision=lax.Precision.HIGHEST,
    ).reshape(chip_count, parent_total // chip_count, 128)
    blocks = own_rows.at[send_ids[0]].get(
        mode="promise_in_bounds", wrap_negative_indices=False
    )
    cell_blocks = own_cells.at[cell_send_ids[0]].get(
        mode="promise_in_bounds", wrap_negative_indices=False
    )
    chip_rows, pool_blocks, pool_cells, parent_moments = exchange(
        own_rows, blocks, cell_blocks, contribution, moment_count
    )
    pool_rows = pool_blocks.reshape(-1, 4, BUCKET)
    pool_table = pool_cells.reshape(-1, 128)
    accel = fields(
        active, local_list, near_list, far_list, chip_rows, pool_rows, pool_table, old_accel
    )
    return (accel, parent_moments.T)


def solution(mesh):
    return jax.shard_map(
        local,
        mesh=mesh,
        in_specs=(
            P(None, ("dom", "sub")),
            P(("dom", "sub")),
            P(None, ("dom", "sub")),
            P("dom"),
            P(("dom", "sub")),
            P(),
            P("dom", None),
            P("dom", None),
            P("dom", None),
            P(("dom", "sub"), None, None),
            P(("dom", "sub"), None, None),
        ),
        out_specs=(P(None, ("dom", "sub")), P(None, "dom")),
        check_vma=False,
    )
```
